512 devices in a mesh: grp: 16 (over y_hi, x, core), seq: 32 (over z, y_lo).
Axes of the slice: x: 4, y: 4 (y_hi: 2, y_lo: 2; y = y_hi * 2 + y_lo), z: 16, core: 2. Of those that a mesh axis runs over, the one named last changes fastest.
Arguments:
- tokens: bfloat16 [32, 64, 128, 512], P(None, 'grp', 'seq'), may hold values from -6 to 6
- cotangent: bfloat16 [32, 64, 128, 512], P(None, 'grp', 'seq'), may hold values from -6 to 6
- gate_weight: bfloat16 [512, 512], replicated, may hold values from -0.25 to 0.25
- first_factor: bfloat16 [4, 32, 32], replicated, may hold values from -1 to 1
- middle_factor: bfloat16 [4, 64, 64], replicated, may hold values from -0.75 to 0.75
- last_factor: bfloat16 [4, 128, 128], replicated, may hold values from -0.5 to 0.5
Outputs:
- d_tokens: bfloat16 [32, 64, 128, 512], P(None, 'grp', 'seq')
- grad_gate: float32 [512, 512], P('seq')
- grad_first: float32 [4, 32, 32], replicated
- grad_middle: float32 [4, 64, 64], P(None, 'grp')
- grad_last: float32 [4, 128, 128], P(None, 'seq')
The draws below stay inside these ranges and needn't reach their ends.
All inputs are finite; a program needn't handle non-finite values.
Results may differ from the reference program's by a relative error of at most 0.0065.
Values may be sent and summed in bfloat16 or wider, within the bound.
A program may use at most 64 MiB of HBM per device.

```python
import math
import jax
import jax.numpy as jnp
from jax import lax

F1 = 32
F2 = 64
F3 = 128
D = 512
HEADS = 4
TOKENS = 262144


def spiked(values, stream_key, source, target, parts, factor):
    owner, partner = [(jnp.arange(values.shape[position]) // (values.shape[position] // parts)).reshape([-1 if axis == position else 1 for axis in range(values.ndim)]) for position in (source, target)]
    chosen = jax.random.permutation(stream_key, parts)[partner]
    strong = (owner == chosen) | (owner == (partner + parts // 2) % parts)
    return jnp.where(strong, factor * values, values)


def level_of(key, dims, cuts, low, top_value):
    def one(position, shards_of):
        draws = jax.random.uniform(jax.random.fold_in(jax.random.fold_in(key, 6), position), (shards_of,), jnp.float32, low / len(cuts), top_value / len(cuts))
        return jnp.repeat(jnp.exp(draws), dims[position] // shards_of).reshape((-1,) + (1,) * (len(dims) - position - 1))

    level = one(*cuts[0])
    for cut in cuts[1:]:
        level = level * one(*cut)
    return level


def bell_draw(rng, extent, width, reach, split=(), held_as=jnp.bfloat16):
    factor_of = level_of(rng, extent, split, -0.22, 0.18) if split else 1.0
    values = jax.random.normal(rng, extent, jnp.float32) * width * factor_of
    return jnp.minimum(jnp.maximum(values, -reach), reach).astype(held_as)


def heavy_noise(rng, dims, spread, bound, shards, heavy, held_as=jnp.bfloat16):
    values = spread * jax.random.normal(rng, dims, jnp.float32)
    if shards:
        values = values * level_of(rng, dims, shards, -0.22, 0.18)
    return jnp.clip(spiked(values, jax.random.fold_in(rng, 3), *heavy), -bound, bound).astype(held_as)


def setup_inputs(seed: int = 0) -> dict:
    key_list = jax.random.split(jax.random.key(seed), 7)
    return {
        "tokens": heavy_noise(key_list[0], (F1, F2, F3, D), 1.0, 6.0, ((1, 16), (2, 32)), (2, 3, 32, 2.75)),
        "cotangent": heavy_noise(key_list[1], (F1, F2, F3, D), 1.0, 6.0, ((1, 16), (2, 32)), (1, 3, 16, 2.0)),
        "gate_weight": bell_draw(key_list[2], (D, D), D ** -0.5, 0.25),
        "first_factor": bell_draw(key_list[3], (HEADS, F1, F1), F1 ** -0.5, 1.0),
        "middle_factor": bell_draw(key_list[4], (HEADS, F2, F2), F2 ** -0.5, 0.75),
        "last_factor": bell_draw(key_list[5], (HEADS, F3, F3), F3 ** -0.5, 0.5),
    }


def headed(values):
    return values.reshape(values.shape[:-1] + (HEADS, values.shape[-1] // HEADS))

def mixing(weights, values, form):
    result = jnp.einsum(form, weights.astype(jnp.float32), headed(values).astype(jnp.float32), precision=lax.Precision.HIGHEST)
    return result.reshape(values.shape)

def contract(left, right, form):
    return jnp.einsum(form, headed(left).astype(jnp.float32), headed(right).astype(jnp.float32), precision=lax.Precision.HIGHEST)

def reference(tokens, cotangent, gate_weight, first_factor, middle_factor, last_factor):
    rows = tokens.reshape(-1, D)
    gate = jax.nn.sigmoid(jnp.dot(rows, gate_weight, preferred_element_type=jnp.float32)).reshape(tokens.shape)
    first_out = mixing(first_factor, tokens, 'hab,bjkhe->ajkhe').astype(jnp.bfloat16)
    last_out = mixing(last_factor, first_out, 'hab,ijbhe->ijahe').astype(jnp.bfloat16)
    mixer = mixing(middle_factor, last_out, 'hab,ibkhe->iakhe').astype(jnp.bfloat16)
    upstream = cotangent.astype(jnp.float32)
    d_mix = (upstream * gate).astype(jnp.bfloat16)
    d_pre = (upstream * mixer.astype(jnp.float32) * gate * (1.0 - gate)).astype(jnp.bfloat16)
    middle_back = mixing(middle_factor, d_mix, 'hba,ibkhe->iakhe').astype(jnp.bfloat16)
    last_back = mixing(last_factor, middle_back, 'hba,ijbhe->ijahe').astype(jnp.bfloat16)
    first_back = mixing(first_factor, last_back, 'hba,bjkhe->ajkhe')
    pre_rows = d_pre.reshape(-1, D)
    d_tokens = (first_back.reshape(-1, D) + jnp.dot(pre_rows, gate_weight.T, preferred_element_type=jnp.float32)).astype(jnp.bfloat16).reshape(tokens.shape)
    factor = 1.0 / math.sqrt(TOKENS)
    grad_gate = jnp.dot(rows.T, pre_rows, preferred_element_type=jnp.float32) * factor
    grad_middle = contract(d_mix, last_out, 'iakhe,ibkhe->hab') * factor
    grad_last = contract(middle_back, first_out, 'ijahe,ijbhe->hab') * factor
    grad_first = contract(last_back, tokens, 'ajkhe,bjkhe->hab') * factor
    return (d_tokens, grad_gate, grad_first, grad_middle, grad_last)
```

```python
import jax
import jax.numpy as jnp
from jax import lax
from jax.experimental import pallas as pl
from jax.experimental.pallas import tpu as pltpu
from jax.sharding import PartitionSpec as P

MESH = pl.DeviceIdType.MESH
BF = jnp.bfloat16
F32 = jnp.float32
SCALE = 1.0 / 512.0
HIGH = lax.Precision.HIGHEST


def mm(a, b):
    return jnp.dot(a, b, preferred_element_type=F32)


def tn(a, b):
    return lax.dot_general(a, b, (((0,), (0,)), ((), ())), preferred_element_type=F32)


def nt(a, b):
    return lax.dot_general(a, b, (((1,), (1,)), ((), ())), preferred_element_type=F32)


def exact(a, b):
    return jnp.dot(a, b, preferred_element_type=F32, precision=HIGH)


def grid2(n, m):
    return (
        lax.broadcasted_iota(jnp.int32, (n, m), 0),
        lax.broadcasted_iota(jnp.int32, (n, m), 1),
    )


def onehot(mask, dtype=BF):
    return jnp.where(mask, 1.0, 0.0).astype(dtype)


def swap_lane(m):
    return ((m >> 5) & 3) * 128 + (m >> 7) * 32 + (m & 31)


def kernel(
    x_ref, c_ref, w_ref, ff_ref, mf_ref, lf_ref,
    dt_ref, gg_ref, gf_ref, gm_ref, gl_ref,
    zs_f, zr_f, zs_d, zr_d, ps_f, pr_f, ps_d, pr_d,
    ps_m, pr_m, zs_m, zr_m, ps_b, pr_b, zs_b, zr_b,
    xtj, ctj, gate, bk, bj, pm, pmt, pkj, aj, ajt, xg, fog, mbg, lbg, mid, loj, dj, dpt, gterm, gfold,
    ps_g, pr_g, zs_g, zr_g, row_g, ar_g,
    ps_s, pr_s, row_s, zr_s, head_s, ar_s,
    zss, zrs, pss, prs,
):
    g = lax.axis_index("grp")
    s = lax.axis_index("seq")
    z = s // 2
    y = s % 2
    p = y * 16 + g
    head = z // 4

    def z_id(t):
        return {"seq": t * 2 + y}

    def p_id(q):
        return {"grp": q % 16, "seq": z * 2 + q // 16}

    bar = pltpu.get_barrier_semaphore()

    def greet_z(d, _):
        pl.semaphore_signal(bar, inc=1, device_id=z_id((z + d) % 16), device_id_type=MESH)
        return _

    def greet_p(d, _):
        pl.semaphore_signal(bar, inc=1, device_id=p_id((p + d) % 32), device_id_type=MESH)
        return _

    lax.fori_loop(1, 16, greet_z, 0)
    lax.fori_loop(1, 32, greet_p, 0)

    def z_send(src, dst, rows, k):
        def step(d, _):
            t = (z + d) % 16
            pltpu.make_async_remote_copy(
                src_ref=src.at[pl.ds(pl.multiple_of(t * rows, rows), rows)],
                dst_ref=dst.at[pl.ds(pl.multiple_of(z * rows, rows), rows)],
                send_sem=zss.at[k], recv_sem=zrs.at[k],
                device_id=z_id(t), device_id_type=MESH,
            ).start()
            return _

        lax.fori_loop(1, 16, step, 0)
        mine = pl.ds(pl.multiple_of(z * rows, rows), rows)
        pltpu.make_async_copy(src.at[mine], dst.at[mine], zrs.at[k]).start()

    def z_cast(src, dst, k):
        def step(d, _):
            t = (z + d) % 16
            pltpu.make_async_remote_copy(
                src_ref=src, dst_ref=dst.at[z],
                send_sem=zss.at[k], recv_sem=zrs.at[k],
                device_id=z_id(t), device_id_type=MESH,
            ).start()
            return _

        lax.fori_loop(1, 16, step, 0)
        pltpu.make_async_copy(src, dst.at[z], zrs.at[k]).start()

    def p_send(src, dst, rows, k):
        def step(d, _):
            q = (p + d) % 32
            pltpu.make_async_remote_copy(
                src_ref=src.at[pl.ds(pl.multiple_of(q * rows, rows), rows)],
                dst_ref=dst.at[pl.ds(pl.multiple_of(p * rows, rows), rows)],
                send_sem=pss.at[k], recv_sem=prs.at[k],
                device_id=p_id(q), device_id_type=MESH,
            ).start()
            return _

        lax.fori_loop(1, 32, step, 0)
        mine = pl.ds(pl.multiple_of(p * rows, rows), rows)
        pltpu.make_async_copy(src.at[mine], dst.at[mine], prs.at[k]).start()

    def got(dst, sem):
        pltpu.make_async_copy(dst, dst, sem).wait()

    def sent(src, n, sem):
        part = src.at[pl.ds(0, n)]
        pltpu.make_async_copy(part, part, sem).wait()

    r, c = grid2(512, 512)
    bk[...] = onehot(r == (c & 31) * 16 + ((c >> 5) & 3) * 4 + (c >> 7))
    xtk = tn(x_ref[...], bk[...]).astype(BF)
    zs_f[0] = xtk[:, :256]
    zs_f[1] = xtk[:, 256:]
    pl.semaphore_wait(bar, 46)
    z_send(zs_f.at[0], zr_f.at[0], 32, 0)
    z_send(zs_f.at[1], zr_f.at[1], 32, 1)

    bj[...] = onehot(r == (c & 31) * 16 + (c >> 7) * 4 + ((c >> 5) & 3))
    xtj[...] = tn(x_ref[...], bj[...]).astype(BF)
    ctj[...] = tn(c_ref[...], bj[...]).astype(BF)
    gt = jax.nn.sigmoid(tn(w_ref[...], xtj[...]))
    gate[...] = gt
    dmix = (ctj[...].astype(F32) * gt).astype(BF)
    zs_d[0] = dmix[:, :256]
    zs_d[1] = dmix[:, 256:]
    z_send(zs_d.at[0], zr_d.at[0], 32, 2)
    z_send(zs_d.at[1], zr_d.at[1], 32, 3)

    pm[...] = onehot(c == (r & 15) * 32 + (r >> 4))
    pmt[...] = onehot(r == (c & 15) * 32 + (c >> 4))
    pkj[...] = onehot(r == swap_lane(c))
    r4, c4 = grid2(128, 32)
    spread4 = onehot((r4 & 31) == c4)
    r1, c1 = grid2(128, 128)
    same4 = (r1 >> 5) == (c1 >> 5)
    ff = ff_ref[head]
    half = mm(spread4, ff).astype(BF)
    fk = jnp.where(same4, nt(half, spread4), 0.0).astype(BF)
    half_t = nt(spread4, ff).astype(BF)
    fkt = jnp.where(same4, nt(half_t, spread4), 0.0).astype(BF)
    qk = onehot(c1 == (r1 & 15) * 8 + ((r1 >> 4) & 1) * 4 + (r1 >> 5))
    lf = lf_ref[head]
    lp = nt(mm(qk, lf).astype(BF), qk).astype(BF)
    lpt = nt(nt(qk, lf).astype(BF), qk).astype(BF)
    rj, cj = grid2(1024, 64)
    spread_j = onehot(cj == ((rj >> 4) & 15) * 4 + (rj >> 8))
    mf = mf_ref[head]
    wide = mm(spread_j, mf).astype(BF)
    wide_t = nt(spread_j, mf).astype(BF)
    for b in range(4):
        rows = slice(b * 256, b * 256 + 256)
        rb, cb = grid2(256, 1024)
        same16 = (rb & 15) == (cb & 15)
        aj[rows] = jnp.where(same16, nt(wide[rows], spread_j), 0.0).astype(BF)
        ajt[rows] = jnp.where(same16, nt(wide_t[rows], spread_j), 0.0).astype(BF)

    for ch in range(2):
        got(zr_f.at[ch], zrs.at[ch])
        ps_f[ch] = mm(pm[...], zr_f[ch]).astype(BF)
        p_send(ps_f.at[ch], pr_f.at[ch], 16, ch)

    for ch in range(2):
        got(pr_f.at[ch], prs.at[ch])
    for k in range(4):
        for yy in range(2):
            at = (k * 2 + yy) * 16
            xg[:, at : at + 16, :] = pr_f[
                k // 2, yy * 256 : yy * 256 + 256, (k % 2) * 128 : (k % 2) * 128 + 128
            ].reshape(16, 16, 128)
    fog[...] = mm(xg[...].reshape(2048, 128), fkt).astype(BF).reshape(16, 128, 128)
    for gi in range(16):
        lbg[gi] = mm(lp, fog[gi]).astype(BF)
    for k in range(4):
        for yy in range(2):
            at = (k * 2 + yy) * 16
            mid[yy * 256 : yy * 256 + 256, k * 128 : k * 128 + 128] = lbg[:, at : at + 16, :].reshape(256, 128)
    lo = mm(mid[...], pkj[...]).astype(BF)
    for j in range(4):
        for yy in range(2):
            loj[j * 256 : j * 256 + 256, yy * 128 : yy * 128 + 128] = lo[
                yy * 256 : yy * 256 + 256, j * 128 : j * 128 + 128
            ]
    for ch in range(2):
        mx = mm(aj[ch * 512 : ch * 512 + 512], loj[...]).astype(BF)
        for j in range(2):
            for yy in range(2):
                ps_m[ch, yy * 256 : yy * 256 + 256, j * 128 : j * 128 + 128] = mx[
                    j * 256 : j * 256 + 256, yy * 128 : yy * 128 + 128
                ]
        p_send(ps_m.at[ch], pr_m.at[ch], 16, 2 + ch)

    def d_relay(ch):
        got(zr_d.at[ch], zrs.at[2 + ch])
        ps_d[ch] = mm(pm[...], zr_d[ch]).astype(BF)
        p_send(ps_d.at[ch], pr_d.at[ch], 16, 4 + ch)

    d_relay(0)
    for ch in range(2):
        got(pr_m.at[ch], prs.at[2 + ch])
        zs_m[ch] = mm(pmt[...], pr_m[ch]).astype(BF)
        z_send(zs_m.at[ch], zr_m.at[ch], 32, 4 + ch)
    d_relay(1)

    for ch in range(2):
        got(pr_d.at[ch], prs.at[4 + ch])
    for j in range(4):
        for yy in range(2):
            dj[j * 256 : j * 256 + 256, yy * 128 : yy * 128 + 128] = pr_d[
                j // 2, yy * 256 : yy * 256 + 256, (j % 2) * 128 : (j % 2) * 128 + 128
            ]
    mb = mm(ajt[...], dj[...]).astype(BF)
    for j in range(4):
        for yy in range(2):
            mid[yy * 256 : yy * 256 + 256, j * 128 : j * 128 + 128] = mb[
                j * 256 : j * 256 + 256, yy * 128 : yy * 128 + 128
            ]
    mbk = mm(mid[...], pkj[...]).astype(BF)
    for k in range(4):
        for yy in range(2):
            at = (k * 2 + yy) * 16
            mbg[:, at : at + 16, :] = mbk[yy * 256 : yy * 256 + 256, k * 128 : k * 128 + 128].reshape(16, 16, 128)
    for gi in range(16):
        lbg[gi] = mm(lpt, mbg[gi]).astype(BF)
    fb = mm(lbg[...].reshape(2048, 128), fk).astype(BF).reshape(16, 128, 128)
    for ch in range(2):
        for k in range(2):
            for yy in range(2):
                at = ((ch * 2 + k) * 2 + yy) * 16
                ps_b[ch, yy * 256 : yy * 256 + 256, k * 128 : k * 128 + 128] = fb[:, at : at + 16, :].reshape(256, 128)
        p_send(ps_b.at[ch], pr_b.at[ch], 16, 6 + ch)

    for b in range(4):
        rb, cb = grid2(256, 1024)
        gram = nt(dj[b * 256 : b * 256 + 256], loj[...])
        gram = jnp.where((rb & 15) == (cb & 15), gram, 0.0)
        gfold[b * 16 : b * 16 + 16] = gram.reshape(16, 16, 1024).sum(axis=1)
    gm = exact(gfold[...], onehot(cj == ((rj >> 4) & 15) * 4 + (rj >> 8), F32))
    gl = jnp.zeros((128, 128), F32)
    gf = jnp.zeros((128, 128), F32)
    for gi in range(16):
        gl = gl + nt(mbg[gi], fog[gi])
        gf = gf + tn(lbg[gi], xg[gi])
    ra, ca = grid2(256, 128)
    pa, aa = ra >> 3, ra & 7
    kc = (ca & 15) * 8 + ((ca >> 4) & 1) * 4 + (ca >> 5)
    sel_l = onehot((aa < 4) & (kc == pa * 4 + aa), F32)
    pack = exact(sel_l, exact(gl, qk.astype(F32)))
    rm, cm = grid2(256, 64)
    jm = (cm & 15) * 4 + (cm >> 4)
    i64r, i64c = grid2(64, 128)
    for odd in range(2):
        sel_m = onehot(((rm & 7) == 4) & (jm == (rm >> 3) * 2 + odd), F32)
        pack = pack + exact(exact(sel_m, gm), onehot(i64c == i64r + 64 * odd, F32))
    fr, fc = grid2(256, 128)
    sel_f = onehot(((fr & 7) == 5) & ((fc & 31) == (fr >> 3)), F32)
    fold_c = onehot((c1 < 32) & ((r1 & 31) == c1), F32)
    pack = pack + exact(exact(sel_f, jnp.where(same4, gf, 0.0)), fold_c)
    ps_s[...] = pack
    p_send(ps_s, pr_s, 8, 8)

    for ch in range(2):
        got(pr_b.at[ch], prs.at[6 + ch])
        zs_b[ch] = mm(pmt[...], pr_b[ch]).astype(BF)
        z_send(zs_b.at[ch], zr_b.at[ch], 32, 6 + ch)

    got(pr_s, prs.at[8])
    row_s[...] = pr_s[...].reshape(32, 8, 128).sum(axis=0)
    z_cast(row_s, zr_s, 8)

    for ch in range(2):
        got(zr_m.at[ch], zrs.at[4 + ch])
        cols = slice(ch * 256, ch * 256 + 256)
        gt = gate[:, cols]
        dpt[:, cols] = (
            ctj[:, cols].astype(F32) * zr_m[ch].astype(F32) * gt * (1.0 - gt)
        ).astype(BF)
    ps_g[...] = nt(mm(pm[...], xtj[...]).astype(BF), dpt[...]).astype(ps_g.dtype)
    p_send(ps_g, pr_g, 16, 9)
    gterm[...] = nt(nt(bj[...], dpt[...]).astype(BF), w_ref[...])

    got(zr_s, zrs.at[8])
    head_s[...] = zr_s[...].reshape(4, 4, 8, 128).sum(axis=1).reshape(32, 128) * SCALE

    def a_send(d, _):
        q = (p + d) % 32
        pltpu.make_async_remote_copy(
            src_ref=head_s, dst_ref=ar_s.at[p],
            send_sem=pss.at[10], recv_sem=prs.at[10],
            device_id=p_id(q), device_id_type=MESH,
        ).start()
        return _

    lax.fori_loop(1, 32, a_send, 0)
    pltpu.make_async_copy(head_s, ar_s.at[p], prs.at[10]).start()

    got(pr_g, prs.at[9])
    tot = pr_g[...].astype(F32).reshape(32, 16, 512).sum(axis=0)
    for t in range(16):
        zs_g[t] = tot[t : t + 1]
    z_send(zs_g, zr_g, 1, 9)

    got(ar_s, prs.at[10])
    for h in range(4):
        gl_ref[h] = ar_s[s, h * 8 : h * 8 + 4, :]
        for a in range(2):
            both = ar_s[g * 2 + a, h * 8 + 4 : h * 8 + 5, :]
            gm_ref[h, a * 2 : a * 2 + 1, :] = both[:, :64]
            gm_ref[h, a * 2 + 1 : a * 2 + 2, :] = both[:, 64:]
        for q in range(32):
            gf_ref[h, q : q + 1, :] = ar_s[q, h * 8 + 5 : h * 8 + 6, :32]

    got(zr_g, zrs.at[9])
    row_g[...] = zr_g[...].sum(axis=0) * SCALE

    def ag_send(d, _):
        q = (g + d) % 16
        pltpu.make_async_remote_copy(
            src_ref=row_g, dst_ref=ar_g.at[g],
            send_sem=pss.at[11], recv_sem=prs.at[11],
            device_id={"grp": q}, device_id_type=MESH,
        ).start()
        return _

    lax.fori_loop(1, 16, ag_send, 0)
    pltpu.make_async_copy(row_g, ar_g.at[g], prs.at[11]).start()

    for ch in range(2):
        got(zr_b.at[ch], zrs.at[6 + ch])
    back = nt(bk[:, :256], zr_b[0]) + nt(bk[:, 256:], zr_b[1])
    dt_ref[...] = (back + gterm[...]).astype(BF)

    got(ar_g, prs.at[11])
    for q in range(16):
        gg_ref[q : q + 1] = ar_g[q]

    for ch in range(2):
        for k, src in enumerate((zs_f, zs_d, zs_m, zs_b)):
            sent(src.at[ch], 480, zss.at[k * 2 + ch])
        for k, src in enumerate((ps_f, ps_m, ps_d, ps_b)):
            sent(src.at[ch], 496, pss.at[k * 2 + ch])
    sent(zr_s, 15, zss.at[8])
    sent(zs_g, 15, zss.at[9])
    sent(ps_s, 248, pss.at[8])
    sent(ps_g, 496, pss.at[9])
    sent(ar_s, 31, pss.at[10])
    sent(ar_g, 15, pss.at[11])


def shards(tokens, cotangent, gate_weight, first_factor, middle_factor, last_factor):
    V = pltpu.VMEM
    big = V((2, 512, 256), BF)
    sq = V((512, 512), BF)
    gtype = BF
    scratch = (
        [big] * 16
        + [sq, sq, V((512, 512), F32), sq, sq, sq, sq, sq, V((1024, 1024), BF), V((1024, 1024), BF)]
        + [V((16, 128, 128), BF)] * 4
        + [sq, V((1024, 256), BF), V((1024, 256), BF), sq, V((512, 512), F32), V((64, 1024), F32)]
        + [V((512, 512), gtype)] * 2
        + [V((16, 1, 512), F32), V((16, 1, 512), F32), V((1, 512), F32), V((16, 1, 512), F32)]
        + [V((256, 128), F32)] * 2
        + [V((8, 128), F32), V((16, 8, 128), F32), V((32, 128), F32), V((32, 32, 128), F32)]
        + [pltpu.SemaphoreType.DMA((12,))] * 4
    )
    vm = pl.BlockSpec(memory_space=V)
    dt, gg, gf, gm, gl = pl.pallas_call(
        kernel,
        name="mixer",
        out_shape=(
            jax.ShapeDtypeStruct((512, 512), BF),
            jax.ShapeDtypeStruct((16, 512), F32),
            jax.ShapeDtypeStruct((4, 32, 32), F32),
            jax.ShapeDtypeStruct((4, 4, 64), F32),
            jax.ShapeDtypeStruct((4, 4, 128), F32),
        ),
        in_specs=[vm] * 6,
        out_specs=(vm,) * 5,
        scratch_shapes=scratch,
        compiler_params=pltpu.CompilerParams(
            collective_id=0, has_side_effects=True, vmem_limit_bytes=60 * 1024 * 1024
        ),
    )(
        tokens.reshape(512, 512), cotangent.reshape(512, 512),
        gate_weight, first_factor, middle_factor, last_factor,
    )
    return dt.reshape(tokens.shape), gg, gf, gm, gl


def solution(mesh):
    in_specs = (P(None, "grp", "seq", None), P(None, "grp", "seq", None), P(), P(), P(), P())
    out_specs = (
        P(None, "grp", "seq", None),
        P("seq", None),
        P(),
        P(None, "grp", None),
        P(None, "seq", None),
    )
    return jax.shard_map(shards, mesh=mesh, in_specs=in_specs, out_specs=out_specs, check_vma=False)
```

```python
import jax
import jax.numpy as jnp
from jax import lax
from jax.experimental import pallas as pl
from jax.experimental.pallas import tpu as pltpu
from jax.sharding import PartitionSpec as P

MESH = pl.DeviceIdType.MESH
BF = jnp.bfloat16
F32 = jnp.float32
SCALE = 1.0 / 512.0
HIGH = lax.Precision.HIGHEST
SPLIT = 8


def mm(a, b):
    return jnp.dot(a, b, preferred_element_type=F32)


def tn(a, b):
    return lax.dot_general(a, b, (((0,), (0,)), ((), ())), preferred_element_type=F32)


def nt(a, b):
    return lax.dot_general(a, b, (((1,), (1,)), ((), ())), preferred_element_type=F32)


def exact(a, b):
    return jnp.dot(a, b, preferred_element_type=F32, precision=HIGH)


def grid2(n, m):
    return (
        lax.broadcasted_iota(jnp.int32, (n, m), 0),
        lax.broadcasted_iota(jnp.int32, (n, m), 1),
    )


def onehot(mask, dtype=BF):
    return jnp.where(mask, 1.0, 0.0).astype(dtype)


def swap_lane(m):
    return ((m >> 5) & 3) * 128 + (m >> 7) * 32 + (m & 31)


def kernel(
    x_in, c_in, w_in, ff_in, mf_in, lf_in,
    dt_ref, gg_ref, sm_ref,
    x_ref, c_ref, w_ref, ff_ref, mf_ref, lf_ref,
    zs_f, zr_f, zs_d, zr_d, ps_f, pr_f, ps_d, pr_d,
    ps_m, pr_m, zs_m, zr_m, ps_b, pr_b, zs_b, zr_b,
    xn, xtj, ctj, gate, bk, bj, pm, pmt, pkj, mid, dpt, xtp, gterm,
    aj, ajt, loj, dj, xg, fog, mbg, lbg, gfold, gacc,
    ps_g, pr_g, zs_g, zr_g, row_g, ar_g,
    ps_s, pr_s, row_s, zr_s, row_l, zr_l, few_s, ar_s, big_s, ar_l,
    zss, zrs, pss, prs, ins,
):
    g = lax.axis_index("grp")
    s = lax.axis_index("seq")
    z = lax.div(s, 2)
    y = lax.rem(s, 2)
    p = y * 16 + g
    head = lax.div(z, 4)

    def z_id(t):
        return {"seq": t * 2 + y}

    def p_id(q):
        return {"grp": lax.rem(q, 16), "seq": z * 2 + lax.div(q, 16)}

    def around(d):
        return lax.rem(z + d, 16)

    loads = [
        pltpu.make_async_copy(src, dst, ins.at[n])
        for n, (src, dst) in enumerate(
            ((x_in, x_ref), (c_in, c_ref), (w_in, w_ref), (ff_in, ff_ref), (mf_in, mf_ref), (lf_in, lf_ref))
        )
    ]
    for load in loads:
        load.start()
    bar = pltpu.get_barrier_semaphore()
    waiting, leaving = {}, []

    def greet_z(d, _):
        pl.semaphore_signal(bar, inc=1, device_id=z_id(around(d)), device_id_type=MESH)
        return _

    def greet_p(d, _):
        pl.semaphore_signal(bar, inc=1, device_id=p_id(lax.rem(p + d, 32)), device_id_type=MESH)
        return _

    lax.fori_loop(1, 16, greet_z, 0)
    lax.fori_loop(1, 32, greet_p, 0)

    def block(t, rows):
        return pl.ds(pl.multiple_of(t * rows, rows), rows)

    def z_send(src, dst, rows, k, first=1, last=16):
        def step(d, _):
            t = around(d * 7)
            pltpu.make_async_remote_copy(
                src_ref=src.at[block(t, rows)], dst_ref=dst.at[block(z, rows)],
                send_sem=zss.at[k], recv_sem=zrs.at[k],
                device_id=z_id(t), device_id_type=MESH,
            ).start()
            return _

        lax.fori_loop(first, last, step, 0)
        if last < 16:
            return
        pltpu.make_async_copy(src.at[block(z, rows)], dst.at[block(z, rows)], zrs.at[k]).start()
        note(dst, zrs, k)
        note_sent(src, 15 * rows, zss.at[k])

    def p_send(src, dst, rows, k):
        def step(d, _):
            q = lax.rem(p + d * 13, 32)
            pltpu.make_async_remote_copy(
                src_ref=src.at[block(q, rows)], dst_ref=dst.at[block(p, rows)],
                send_sem=pss.at[k], recv_sem=prs.at[k],
                device_id=p_id(q), device_id_type=MESH,
            ).start()
            return _

        lax.fori_loop(1, 32, step, 0)
        pltpu.make_async_copy(src.at[block(p, rows)], dst.at[block(p, rows)], prs.at[k]).start()
        note(dst, prs, k)
        note_sent(src, 31 * rows, pss.at[k])

    def got(dst, sem, n):
        pltpu.make_async_copy(dst, dst, sem.at[n]).wait()
        waiting.pop((id(sem), n), None)

    def note(dst, sem, n):
        waiting[(id(sem), n)] = lambda: got(dst, sem, n)

    def note_sent(src, n, sem):
        part = src.at[pl.ds(0, n)]
        leaving.append(pltpu.make_async_copy(part, part, sem))

    def finish():
        for step in list(waiting.values()):
            step()
        for copy in leaving:
            copy.wait()

    def lanes(j):
        return slice(j * 128, j * 128 + 128)

    def half(yy):
        return slice(yy * 256, yy * 256 + 256)

    r, c = grid2(512, 512)
    bk[...] = onehot(r == (c & 31) * 16 + ((c >> 5) & 3) * 4 + (c >> 7))
    loads[0].wait()
    xn[...] = x_ref[...].reshape(512, 512)
    xtk = tn(xn[...], bk[...]).astype(BF)
    for k in range(4):
        zs_f[k] = xtk[:, lanes(k)]
    pl.semaphore_wait(bar, 46)
    for k in range(4):
        z_send(zs_f.at[k], zr_f.at[k], 32, k)

    bj[...] = onehot(r == (c & 31) * 16 + (c >> 7) * 4 + ((c >> 5) & 3))
    xtj[...] = tn(xn[...], bj[...]).astype(BF)
    loads[1].wait()
    ctj[...] = tn(c_ref[...].reshape(512, 512), bj[...]).astype(BF)
    loads[2].wait()
    gt = jax.nn.sigmoid(tn(w_ref[...], xtj[...]))
    gate[...] = gt
    dmix = (ctj[...].astype(F32) * gt).astype(BF)
    for j in range(4):
        zs_d[j] = dmix[:, lanes(j)]
    for j in range(4):
        z_send(zs_d.at[j], zr_d.at[j], 32, 4 + j)

    pm[...] = onehot(c == (r & 15) * 32 + (r >> 4))
    pmt[...] = onehot(r == (c & 15) * 32 + (c >> 4))
    pkj[...] = onehot(r == swap_lane(c))
    r4, c4 = grid2(128, 32)
    spread4 = onehot((r4 & 31) == c4)
    r1, c1 = grid2(128, 128)
    same4 = (r1 >> 5) == (c1 >> 5)
    for load in loads[3:]:
        load.wait()
    ff = ff_ref[head]
    fk = jnp.where(same4, nt(mm(spread4, ff).astype(BF), spread4), 0.0).astype(BF)
    fkt = jnp.where(same4, nt(nt(spread4, ff).astype(BF), spread4), 0.0).astype(BF)
    qk = onehot(c1 == (r1 & 15) * 8 + ((r1 >> 4) & 1) * 4 + (r1 >> 5))
    lf = lf_ref[head]
    lp = nt(mm(qk, lf).astype(BF), qk).astype(BF)
    lpt = nt(nt(qk, lf).astype(BF), qk).astype(BF)
    rj, cj = grid2(1024, 64)
    spread_j = onehot(cj == ((rj >> 4) & 15) * 4 + (rj >> 8))
    mf = mf_ref[head]
    wide = mm(spread_j, mf).astype(BF)
    wide_t = nt(spread_j, mf).astype(BF)
    for b in range(4):
        rb, cb = grid2(256, 1024)
        same16 = (rb & 15) == (cb & 15)
        aj[half(b)] = jnp.where(same16, nt(wide[half(b)], spread_j), 0.0).astype(BF)
        ajt[half(b)] = jnp.where(same16, nt(wide_t[half(b)], spread_j), 0.0).astype(BF)
    xtp[...] = mm(pm[...], xtj[...]).astype(BF)

    for k in range(4):
        got(zr_f.at[k], zrs, k)
        ps_f[k] = mm(pm[...], zr_f[k]).astype(BF)
        p_send(ps_f.at[k], pr_f.at[k], 16, k)

    for k in range(4):
        got(pr_f.at[k], prs, k)
        fo = mm(pr_f[k], fkt).astype(BF)
        for yy in range(2):
            at = (k * 2 + yy) * 16
            fog[:, at : at + 16, :] = fo[half(yy)].reshape(16, 16, 128)
    for gi in range(16):
        lbg[gi] = mm(lp, fog[gi]).astype(BF)
    for k in range(4):
        for yy in range(2):
            at = (k * 2 + yy) * 16
            mid[half(yy), lanes(k)] = lbg[:, at : at + 16, :].reshape(256, 128)
    lo = mm(mid[...], pkj[...]).astype(BF)
    for j in range(4):
        for yy in range(2):
            loj[half(j), lanes(yy)] = lo[half(yy), lanes(j)]
    for j in range(4):
        mx = mm(aj[half(j)], loj[...]).astype(BF)
        for yy in range(2):
            ps_m[j, half(yy)] = mx[:, lanes(yy)]
        p_send(ps_m.at[j], pr_m.at[j], 16, 4 + j)

    def d_relay(j):
        got(zr_d.at[j], zrs, 4 + j)
        ps_d[j] = mm(pm[...], zr_d[j]).astype(BF)
        p_send(ps_d.at[j], pr_d.at[j], 16, 8 + j)

    def m_relay(j):
        got(pr_m.at[j], prs, 4 + j)
        zs_m[j] = mm(pmt[...], pr_m[j]).astype(BF)
        z_send(zs_m.at[j], zr_m.at[j], 32, 8 + j)

    d_relay(0)
    d_relay(1)
    m_relay(0)
    d_relay(2)
    m_relay(1)
    m_relay(2)
    d_relay(3)
    m_relay(3)

    for j in range(4):
        got(pr_d.at[j], prs, 8 + j)
        for yy in range(2):
            dj[half(j), lanes(yy)] = pr_d[j, half(yy)]
    mb = mm(ajt[...], dj[...]).astype(BF)
    for j in range(4):
        for yy in range(2):
            mid[half(yy), lanes(j)] = mb[half(j), lanes(yy)]
    mbk = mm(mid[...], pkj[...]).astype(BF)
    for k in range(4):
        for yy in range(2):
            at = (k * 2 + yy) * 16
            mbg[:, at : at + 16, :] = mbk[half(yy), lanes(k)].reshape(16, 16, 128)
    for gi in range(16):
        lbg[gi] = mm(lpt, mbg[gi]).astype(BF)
    fb = mm(lbg[...].reshape(2048, 128), fk).astype(BF).reshape(16, 128, 128)
    for k in range(4):
        for yy in range(2):
            at = (k * 2 + yy) * 16
            ps_b[k, half(yy)] = fb[:, at : at + 16, :].reshape(256, 128)
    for k in range(2):
        p_send(ps_b.at[k], pr_b.at[k], 16, 12 + k)

    for k in range(4):
        for yy in range(2):
            at = (k * 2 + yy) * 16
            xg[:, at : at + 16, :] = pr_f[k, half(yy)].reshape(16, 16, 128)
    for b in range(4):
        rb, cb = grid2(256, 1024)
        gram = nt(dj[half(b)], loj[...])
        gram = jnp.where((rb & 15) == (cb & 15), gram, 0.0)
        gfold[b * 16 : b * 16 + 16] = gram.reshape(16, 16, 1024).sum(axis=1)
    gm = exact(gfold[...], onehot(cj == ((rj >> 4) & 15) * 4 + (rj >> 8), F32))
    gl = jnp.zeros((128, 128), F32)
    gf = jnp.zeros((128, 128), F32)
    for gi in range(16):
        gl = gl + nt(mbg[gi], fog[gi])
        gf = gf + tn(lbg[gi], xg[gi])
    ra, ca = grid2(256, 128)
    pa, aa = ra >> 3, ra & 7
    kc = (ca & 15) * 8 + ((ca >> 4) & 1) * 4 + (ca >> 5)
    sel_l = onehot((aa < 4) & (kc == pa * 4 + aa), F32)
    pack = exact(sel_l, exact(gl, qk.astype(F32)))
    rm, cm = grid2(256, 64)
    jm = (cm & 15) * 4 + (cm >> 4)
    i64r, i64c = grid2(64, 128)
    for odd in range(2):
        sel_m = onehot(((rm & 7) == 4) & (jm == (rm >> 3) * 2 + odd), F32)
        pack = pack + exact(exact(sel_m, gm), onehot(i64c == i64r + 64 * odd, F32))
    sel_f = onehot((aa == 5) & ((ca & 31) == pa), F32)
    fold_c = onehot(c1 == (r1 & 31) + head * 32, F32)
    pack = pack + exact(exact(sel_f, jnp.where(same4, gf, 0.0)), fold_c)
    ps_s[...] = pack
    p_send(ps_s, pr_s, 8, 16)
    for k in range(2, 4):
        p_send(ps_b.at[k], pr_b.at[k], 16, 12 + k)

    def b_relay(k):
        got(pr_b.at[k], prs, 12 + k)
        zs_b[k] = mm(pmt[...], pr_b[k]).astype(BF)
        z_send(zs_b.at[k], zr_b.at[k], 32, 12 + k)

    def gate_share(j):
        got(zr_m.at[j], zrs, 8 + j)
        gt = gate[:, lanes(j)]
        dpre = (ctj[:, lanes(j)].astype(F32) * zr_m[j].astype(F32) * gt * (1.0 - gt)).astype(BF)
        dpt[:, lanes(j)] = dpre
        share = nt(xtp[:, lanes(j)], dpre)
        if j == 0:
            gacc[...] = share
        elif j < 3:
            gacc[...] += share
        else:
            ps_g[...] = (gacc[...] + share).astype(BF)

    b_relay(0)
    gate_share(0)
    gate_share(1)
    b_relay(1)
    gate_share(2)
    gate_share(3)
    p_send(ps_g, pr_g, 16, 17)
    b_relay(2)

    owner = lax.div(p, 2) == z
    side = lax.rem(p, 2)
    got(pr_s, prs, 16)
    row = pr_s[...].reshape(32, 8, 128).sum(axis=0)
    row_s[...] = row[4:6]
    row_l[...] = row[0:4]

    def row_copy():
        return pltpu.make_async_remote_copy(
            src_ref=row_l, dst_ref=zr_l.at[z], send_sem=zss.at[18], recv_sem=zrs.at[18],
            device_id=z_id(lax.div(p, 2)), device_id_type=MESH,
        )

    @pl.when(owner)
    def _():
        pltpu.make_async_copy(row_l, zr_l.at[z], zrs.at[18]).start()

    @pl.when(jnp.logical_not(owner))
    def _():
        row_copy().start()

    def cast(d, _):
        pltpu.make_async_remote_copy(
            src_ref=row_s, dst_ref=zr_s.at[z], send_sem=zss.at[16], recv_sem=zrs.at[16],
            device_id=z_id(around(d)), device_id_type=MESH,
        ).start()
        return _

    lax.fori_loop(1, 16, cast, 0)
    pltpu.make_async_copy(row_s, zr_s.at[z], zrs.at[16]).start()
    note(zr_s, zrs, 16)
    note_sent(zr_s, 15, zss.at[16])

    got(pr_b.at[3], prs, 15)
    zs_b[3] = mm(pmt[...], pr_b[3]).astype(BF)
    z_send(zs_b.at[3], zr_b.at[3], 32, 15, 1, SPLIT)
    gterm[...] = nt(nt(bj[...], dpt[...]).astype(BF), w_ref[...])

    got(pr_g, prs, 17)
    tot = pr_g[...].astype(F32).reshape(32, 16, 512).sum(axis=0)
    for t in range(16):
        zs_g[t] = tot[t : t + 1]
    z_send(zs_g, zr_g, 1, 17)
    z_send(zs_b.at[3], zr_b.at[3], 32, 15, SPLIT, 16)

    got(zr_s, zrs, 16)
    for h in range(4):
        few_s[h : h + 1] = zr_s[4 * h : 4 * h + 4, 0:1, :].sum(axis=0) * SCALE
    few_s[4:5] = zr_s[:, 1:2, :].sum(axis=0) * SCALE
    few_s[5:8] = jnp.zeros((3, 128), F32)

    def few(d, _):
        q = lax.rem(p + d * 13, 32)
        pltpu.make_async_remote_copy(
            src_ref=few_s, dst_ref=ar_s.at[p], send_sem=pss.at[18], recv_sem=prs.at[18],
            device_id=p_id(q), device_id_type=MESH,
        ).start()
        return _

    lax.fori_loop(1, 32, few, 0)
    pltpu.make_async_copy(few_s, ar_s.at[p], prs.at[18]).start()
    note_sent(ar_s, 31, pss.at[18])

    def big_copy(t):
        return pltpu.make_async_remote_copy(
            src_ref=big_s, dst_ref=ar_l, send_sem=pss.at[19], recv_sem=prs.at[19],
            device_id={"grp": t, "seq": z * 2 + side}, device_id_type=MESH,
        )

    @pl.when(owner)
    def _():
        got(zr_l, zrs, 18)
        for h in range(4):
            big_s[h * 4 : h * 4 + 4] = zr_l[4 * h : 4 * h + 4].sum(axis=0) * SCALE

        def step(d, _):
            big_copy(lax.rem(g + d, 16)).start()
            return _

        lax.fori_loop(1, 16, step, 0)

    @pl.when(owner & (side == y))
    def _():
        pltpu.make_async_copy(big_s, ar_l, prs.at[19]).start()

    @pl.when(owner & (side != y))
    def _():
        big_copy(g).start()

    got(ar_l, prs, 19)
    sm_ref[0:16] = ar_l[...]
    got(ar_s, prs, 18)
    for a in range(2):
        sm_ref[16 + a * 4 : 20 + a * 4] = ar_s[g * 2 + a, 0:4, :]
    for q in range(32):
        sm_ref[24 + q : 25 + q] = ar_s[q, 4:5, :]

    got(zr_g, zrs, 17)
    row_g[...] = zr_g[...].sum(axis=0) * SCALE

    def rows_out(d, _):
        pltpu.make_async_remote_copy(
            src_ref=row_g, dst_ref=ar_g.at[g], send_sem=pss.at[20], recv_sem=prs.at[20],
            device_id={"grp": lax.rem(g + d, 16)}, device_id_type=MESH,
        ).start()
        return _

    lax.fori_loop(1, 16, rows_out, 0)
    pltpu.make_async_copy(row_g, ar_g.at[g], prs.at[20]).start()
    note_sent(ar_g, 15, pss.at[20])

    for k in range(3):
        got(zr_b.at[k], zrs, 12 + k)
        gterm[...] += nt(bk[:, lanes(k)], zr_b[k])
    got(zr_b.at[3], zrs, 15)
    dt_ref[...] = (gterm[...] + nt(bk[:, lanes(3)], zr_b[3])).astype(BF)

    got(ar_g, prs, 20)
    for q in range(16):
        gg_ref[q : q + 1] = ar_g[q]

    finish()

    @pl.when(jnp.logical_not(owner))
    def _():
        row_copy().wait_send()

    @pl.when(owner)
    def _():
        for _i in range(15):
            got(big_s, pss, 19)

    @pl.when(owner & (side != y))
    def _():
        got(big_s, pss, 19)


def unpack(dt_ref, gg_ref, sm_ref, d_ref, g_ref, f_ref, m_ref, l_ref):
    d_ref[...] = dt_ref[...].reshape(32, 4, 4, 512)
    g_ref[...] = gg_ref[...]
    for h in range(4):
        l_ref[h] = sm_ref[h * 4 : h * 4 + 4]
        for a in range(2):
            m_ref[h, a * 2 : a * 2 + 1] = sm_ref[16 + a * 4 + h : 17 + a * 4 + h, :64]
            m_ref[h, a * 2 + 1 : a * 2 + 2] = sm_ref[16 + a * 4 + h : 17 + a * 4 + h, 64:]
        f_ref[h] = sm_ref[24:56, h * 32 : h * 32 + 32]


def shards(tokens, cotangent, gate_weight, first_factor, middle_factor, last_factor):
    V = pltpu.VMEM
    big = V((4, 512, 128), BF)
    sq = V((512, 512), BF)
    scratch = (
        [V(a.shape, BF) for a in (tokens, cotangent, gate_weight, first_factor, middle_factor, last_factor)]
        + [big] * 16
        + [sq, sq, sq, V((512, 512), F32), sq, sq, sq, sq, sq, sq, sq, sq, V((512, 512), F32)]
        + [V((1024, 1024), BF)] * 2
        + [V((1024, 256), BF)] * 2
        + [V((16, 128, 128), BF)] * 4
        + [V((64, 1024), F32), V((512, 512), F32)]
        + [sq, sq, V((16, 1, 512), F32), V((16, 1, 512), F32), V((1, 512), F32), V((16, 1, 512), F32)]
        + [V((256, 128), F32)] * 2
        + [V((2, 128), F32), V((16, 2, 128), F32), V((4, 128), F32), V((16, 4, 128), F32), V((8, 128), F32), V((32, 8, 128), F32)]
        + [V((16, 128), F32)] * 2
        + [pltpu.SemaphoreType.DMA((n,)) for n in (19, 19, 21, 21, 6)]
    )
    vm = pl.BlockSpec(memory_space=V)
    dt, gg, sm = pl.pallas_call(
        kernel,
        name="mixer",
        out_shape=(
            jax.ShapeDtypeStruct((512, 512), BF),
            jax.ShapeDtypeStruct((16, 512), F32),
            jax.ShapeDtypeStruct((56, 128), F32),
        ),
        in_specs=[pl.BlockSpec(memory_space=pl.ANY)] * 6,
        out_specs=(vm,) * 3,
        scratch_shapes=scratch,
        compiler_params=pltpu.CompilerParams(
            collective_id=0, has_side_effects=True, vmem_limit_bytes=60 * 1024 * 1024
        ),
    )(tokens, cotangent, gate_weight, first_factor, middle_factor, last_factor)
    return pl.pallas_call(
        unpack,
        name="unpack",
        out_shape=(
            jax.ShapeDtypeStruct((32, 4, 4, 512), BF),
            jax.ShapeDtypeStruct((16, 512), F32),
            jax.ShapeDtypeStruct((4, 32, 32), F32),
            jax.ShapeDtypeStruct((4, 4, 64), F32),
            jax.ShapeDtypeStruct((4, 4, 128), F32),
        ),
        in_specs=[vm] * 3,
        out_specs=(vm,) * 5,
    )(dt, gg, sm)


def solution(mesh):
    in_specs = (P(None, "grp", "seq", None), P(None, "grp", "seq", None), P(), P(), P(), P())
    out_specs = (
        P(None, "grp", "seq", None),
        P("seq", None),
        P(),
        P(None, "grp", None),
        P(None, "seq", None),
    )
    return jax.shard_map(shards, mesh=mesh, in_specs=in_specs, out_specs=out_specs, check_vma=False)
```

```python
import jax
import jax.numpy as jnp
from jax import lax
from jax.experimental import pallas as pl
from jax.experimental.pallas import tpu as pltpu
from jax.sharding import PartitionSpec as P

MESH = pl.DeviceIdType.MESH
BF = jnp.bfloat16
F32 = jnp.float32
SCALE = 1.0 / 512.0
HIGH = lax.Precision.HIGHEST
SPLIT = 11


def mm(a, b):
    return jnp.dot(a, b, preferred_element_type=F32)


def tn(a, b):
    return lax.dot_general(a, b, (((0,), (0,)), ((), ())), preferred_element_type=F32)


def nt(a, b):
    return lax.dot_general(a, b, (((1,), (1,)), ((), ())), preferred_element_type=F32)


def exact(a, b):
    return jnp.dot(a, b, preferred_element_type=F32, precision=HIGH)


def grid2(n, m):
    return (
        lax.broadcasted_iota(jnp.int32, (n, m), 0),
        lax.broadcasted_iota(jnp.int32, (n, m), 1),
    )


def onehot(mask, dtype=BF):
    return jnp.where(mask, 1.0, 0.0).astype(dtype)


def swap_lane(m):
    return ((m >> 5) & 3) * 128 + (m >> 7) * 32 + (m & 31)


def kernel(
    x_in, c_in, w_in, ff_in, mf_in, lf_in,
    dt_ref, gg_ref, sm_ref,
    x_ref, c_ref, w_ref, ff_ref, mf_ref, lf_ref,
    zs_f, zr_f, zs_d, zr_d, ps_f, pr_f, ps_d, pr_d,
    ps_m, pr_m, zs_m, zr_m, ps_b, pr_b, zs_b, zr_b,
    xn, xtj, ctj, gate, bk, bj, pm, pmt, pkj, mid, dpt, xtp, gterm,
    aj, ajt, loj, dj, xg, fog, mbg, lbg, gfold, gacc,
    ps_g, pr_g, zs_g, zr_g, row_g, ar_g,
    ps_s, pr_s, row_s, zr_s, row_l, zr_l, few_s, ar_s, big_s, ar_l,
    zss, zrs, pss, prs, ins, far,
):
    g = lax.axis_index("grp")
    s = lax.axis_index("seq")
    z = lax.div(s, 2)
    y = lax.rem(s, 2)
    p = y * 16 + g
    head = lax.div(z, 4)

    def z_id(t):
        return {"seq": t * 2 + y}

    def p_id(q):
        return {"grp": lax.rem(q, 16), "seq": z * 2 + lax.div(q, 16)}

    def around(d):
        return lax.rem(z + d, 16)

    loads = [
        pltpu.make_async_copy(src, dst, ins.at[n])
        for n, (src, dst) in enumerate(
            ((x_in, x_ref), (c_in, c_ref), (w_in, w_ref), (ff_in, ff_ref), (mf_in, mf_ref), (lf_in, lf_ref))
        )
    ]
    for load in loads:
        load.start()
    bar = pltpu.get_barrier_semaphore()
    waiting, leaving = {}, []

    def greet_z(d, _):
        pl.semaphore_signal(bar, inc=1, device_id=z_id(around(d)), device_id_type=MESH)
        return _

    def greet_p(d, _):
        pl.semaphore_signal(bar, inc=1, device_id=p_id(lax.rem(p + d, 32)), device_id_type=MESH)
        return _

    lax.fori_loop(1, 5, greet_z, 0)
    lax.fori_loop(12, 16, greet_z, 0)
    lax.fori_loop(1, 32, greet_p, 0)

    def block(t, rows):
        return pl.ds(pl.multiple_of(t * rows, rows), rows)

    def z_send(src, dst, rows, k, first=1, last=16, stop=None):
        def step(d, _):
            t = around(d * 7)
            pltpu.make_async_remote_copy(
                src_ref=src.at[block(t, rows)], dst_ref=dst.at[block(z, rows)],
                send_sem=zss.at[k], recv_sem=zrs.at[k],
                device_id=z_id(t), device_id_type=MESH,
            ).start()
            return _

        lax.fori_loop(first, last if stop is None else stop, step, 0)
        if last < 16:
            return
        pltpu.make_async_copy(src.at[block(z, rows)], dst.at[block(z, rows)], zrs.at[k]).start()
        note(dst, zrs, k)
        note_sent(src, 15 * rows, zss.at[k])

    def p_send(src, dst, rows, k):
        def step(d, _):
            q = lax.rem(p + d * 13, 32)
            pltpu.make_async_remote_copy(
                src_ref=src.at[block(q, rows)], dst_ref=dst.at[block(p, rows)],
                send_sem=pss.at[k], recv_sem=prs.at[k],
                device_id=p_id(q), device_id_type=MESH,
            ).start()
            return _

        lax.fori_loop(1, 32, step, 0)
        pltpu.make_async_copy(src.at[block(p, rows)], dst.at[block(p, rows)], prs.at[k]).start()
        note(dst, prs, k)
        note_sent(src, 31 * rows, pss.at[k])

    def got(dst, sem, n):
        pltpu.make_async_copy(dst, dst, sem.at[n]).wait()
        waiting.pop((id(sem), n), None)

    def note(dst, sem, n):
        waiting[(id(sem), n)] = lambda: got(dst, sem, n)

    def note_sent(src, n, sem):
        part = src.at[pl.ds(0, n)]
        leaving.append(pltpu.make_async_copy(part, part, sem))

    def finish():
        for step in list(waiting.values()):
            step()
        for copy in leaving:
            copy.wait()

    def z_pair(src, dst, k):
        def step(d, _):
            for t in (around(d), around(16 - d)):
                pltpu.make_async_remote_copy(
                    src_ref=src.at[block(t, 32)], dst_ref=dst.at[block(z, 32)],
                    send_sem=zss.at[k], recv_sem=zrs.at[k],
                    device_id=z_id(t), device_id_type=MESH,
                ).start()
            return _

        return step

    def pair(k):
        return slice(k * 256, k * 256 + 256)

    def lanes(j):
        return slice(j * 128, j * 128 + 128)

    def half(yy):
        return slice(yy * 256, yy * 256 + 256)

    r, c = grid2(512, 512)
    bk[...] = onehot(r == (c & 31) * 16 + ((c >> 5) & 3) * 4 + (c >> 7))
    loads[0].wait()
    xn[...] = x_ref[...].reshape(512, 512)
    xtk = tn(xn[...], bk[...]).astype(BF)
    for k in range(4):
        zs_f[k] = xtk[:, lanes(k)]
    pl.semaphore_wait(bar, 39)
    pl.semaphore_signal(far.at[0], inc=1, device_id=z_id(around(4)), device_id_type=MESH)
    pl.semaphore_signal(far.at[1], inc=1, device_id=z_id(around(12)), device_id_type=MESH)
    for k in range(2):
        lax.fori_loop(1, 5, z_pair(zs_f.at[k], zr_f.at[k], k), 0)
    pl.semaphore_wait(far.at[0], 1)
    pl.semaphore_wait(far.at[1], 1)
    for k in range(2):
        lax.fori_loop(5, 8, z_pair(zs_f.at[k], zr_f.at[k], k), 0)
        z_send(zs_f.at[k], zr_f.at[k], 32, k, 8, 16, 9)
    for k in range(2, 4):
        z_send(zs_f.at[k], zr_f.at[k], 32, k)

    bj[...] = onehot(r == (c & 31) * 16 + (c >> 7) * 4 + ((c >> 5) & 3))
    xtj[...] = tn(xn[...], bj[...]).astype(BF)
    loads[1].wait()
    ctj[...] = tn(c_ref[...].reshape(512, 512), bj[...]).astype(BF)
    loads[2].wait()
    gt = jax.nn.sigmoid(tn(w_ref[...], xtj[...]))
    gate[...] = gt
    dmix = (ctj[...].astype(F32) * gt).astype(BF)
    for k in range(2):
        zs_d[k] = dmix[:, pair(k)]
    for k in range(2):
        z_send(zs_d.at[k], zr_d.at[k], 32, 4 + k)

    pm[...] = onehot(c == (r & 15) * 32 + (r >> 4))
    pmt[...] = onehot(r == (c & 15) * 32 + (c >> 4))
    pkj[...] = onehot(r == swap_lane(c))
    r4, c4 = grid2(128, 32)
    spread4 = onehot((r4 & 31) == c4)
    r1, c1 = grid2(128, 128)
    same4 = (r1 >> 5) == (c1 >> 5)
    for load in loads[3:]:
        load.wait()
    ff = ff_ref[head]
    fk = jnp.where(same4, nt(mm(spread4, ff).astype(BF), spread4), 0.0).astype(BF)
    fkt = jnp.where(same4, nt(nt(spread4, ff).astype(BF), spread4), 0.0).astype(BF)
    qk = onehot(c1 == (r1 & 15) * 8 + ((r1 >> 4) & 1) * 4 + (r1 >> 5))
    lf = lf_ref[head]
    lp = nt(mm(qk, lf).astype(BF), qk).astype(BF)
    lpt = nt(nt(qk, lf).astype(BF), qk).astype(BF)
    rj, cj = grid2(1024, 64)
    spread_j = onehot(cj == ((rj >> 4) & 15) * 4 + (rj >> 8))
    mf = mf_ref[head]
    wide = mm(spread_j, mf).astype(BF)
    wide_t = nt(spread_j, mf).astype(BF)
    for b in range(4):
        rb, cb = grid2(256, 1024)
        same16 = (rb & 15) == (cb & 15)
        aj[half(b)] = jnp.where(same16, nt(wide[half(b)], spread_j), 0.0).astype(BF)
        ajt[half(b)] = jnp.where(same16, nt(wide_t[half(b)], spread_j), 0.0).astype(BF)
    xtp[...] = mm(pm[...], xtj[...]).astype(BF)

    for k in range(4):
        got(zr_f.at[k], zrs, k)
        ps_f[k] = mm(pm[...], zr_f[k]).astype(BF)
        p_send(ps_f.at[k], pr_f.at[k], 16, k)

    for k in range(4):
        got(pr_f.at[k], prs, k)
        fo = mm(pr_f[k], fkt).astype(BF)
        for yy in range(2):
            at = (k * 2 + yy) * 16
            fog[:, at : at + 16, :] = fo[half(yy)].reshape(16, 16, 128)
    for gi in range(16):
        lbg[gi] = mm(lp, fog[gi]).astype(BF)
    for k in range(4):
        for yy in range(2):
            at = (k * 2 + yy) * 16
            mid[half(yy), lanes(k)] = lbg[:, at : at + 16, :].reshape(256, 128)
    lo = mm(mid[...], pkj[...]).astype(BF)
    for j in range(4):
        for yy in range(2):
            loj[half(j), lanes(yy)] = lo[half(yy), lanes(j)]
    for j in range(4):
        mx = mm(aj[half(j)], loj[...]).astype(BF)
        for yy in range(2):
            ps_m[j, half(yy)] = mx[:, lanes(yy)]
        p_send(ps_m.at[j], pr_m.at[j], 16, 4 + j)

    def d_relay(j):
        got(zr_d.at[j], zrs, 4 + j)
        ps_d[j] = mm(pm[...], zr_d[j]).astype(BF)
        p_send(ps_d.at[j], pr_d.at[j], 16, 8 + j)

    def m_relay(j):
        got(pr_m.at[j], prs, 4 + j)
        zs_m[j] = mm(pmt[...], pr_m[j]).astype(BF)
        z_send(zs_m.at[j], zr_m.at[j], 32, 8 + j)

    d_relay(0)
    m_relay(0)
    m_relay(1)
    m_relay(2)
    d_relay(1)
    m_relay(3)

    for k in range(2):
        got(pr_d.at[k], prs, 8 + k)
        for j in range(2):
            for yy in range(2):
                dj[half(2 * k + j), lanes(yy)] = pr_d[k, half(yy), lanes(j)]
    mb = mm(ajt[...], dj[...]).astype(BF)
    for j in range(4):
        for yy in range(2):
            mid[half(yy), lanes(j)] = mb[half(j), lanes(yy)]
    mbk = mm(mid[...], pkj[...]).astype(BF)
    for k in range(4):
        for yy in range(2):
            at = (k * 2 + yy) * 16
            mbg[:, at : at + 16, :] = mbk[half(yy), lanes(k)].reshape(16, 16, 128)
    for gi in range(16):
        lbg[gi] = mm(lpt, mbg[gi]).astype(BF)
    fb = mm(lbg[...].reshape(2048, 128), fk).astype(BF).reshape(16, 128, 128)
    for k in range(4):
        for yy in range(2):
            at = (k * 2 + yy) * 16
            ps_b[k // 2, half(yy), lanes(k % 2)] = fb[:, at : at + 16, :].reshape(256, 128)
    p_send(ps_b.at[0], pr_b.at[0], 16, 12)

    for k in range(4):
        for yy in range(2):
            at = (k * 2 + yy) * 16
            xg[:, at : at + 16, :] = pr_f[k, half(yy)].reshape(16, 16, 128)
    for b in range(4):
        rb, cb = grid2(256, 1024)
        gram = nt(dj[half(b)], loj[...])
        gram = jnp.where((rb & 15) == (cb & 15), gram, 0.0)
        gfold[b * 16 : b * 16 + 16] = gram.reshape(16, 16, 1024).sum(axis=1)
    gm = exact(gfold[...], onehot(cj == ((rj >> 4) & 15) * 4 + (rj >> 8), F32))
    gl = jnp.zeros((128, 128), F32)
    gf = jnp.zeros((128, 128), F32)
    for gi in range(16):
        gl = gl + nt(mbg[gi], fog[gi])
        gf = gf + tn(lbg[gi], xg[gi])
    ra, ca = grid2(256, 128)
    pa, aa = ra >> 3, ra & 7
    kc = (ca & 15) * 8 + ((ca >> 4) & 1) * 4 + (ca >> 5)
    sel_l = onehot((aa < 4) & (kc == pa * 4 + aa), F32)
    pack = exact(sel_l, exact(gl, qk.astype(F32)))
    rm, cm = grid2(256, 64)
    jm = (cm & 15) * 4 + (cm >> 4)
    i64r, i64c = grid2(64, 128)
    for odd in range(2):
        sel_m = onehot(((rm & 7) == 4) & (jm == (rm >> 3) * 2 + odd), F32)
        pack = pack + exact(exact(sel_m, gm), onehot(i64c == i64r + 64 * odd, F32))
    sel_f = onehot((aa == 5) & ((ca & 31) == pa), F32)
    fold_c = onehot(c1 == (r1 & 31) + head * 32, F32)
    pack = pack + exact(exact(sel_f, jnp.where(same4, gf, 0.0)), fold_c)
    ps_s[...] = pack
    p_send(ps_s, pr_s, 8, 16)
    p_send(ps_b.at[1], pr_b.at[1], 16, 13)

    def gate_share(j):
        got(zr_m.at[j], zrs, 8 + j)
        gt = gate[:, lanes(j)]
        dpre = (ctj[:, lanes(j)].astype(F32) * zr_m[j].astype(F32) * gt * (1.0 - gt)).astype(BF)
        dpt[:, lanes(j)] = dpre
        share = nt(xtp[:, lanes(j)], dpre)
        if j == 0:
            gacc[...] = share
        elif j < 3:
            gacc[...] += share
        else:
            ps_g[...] = (gacc[...] + share).astype(BF)

    got(pr_b.at[0], prs, 12)
    zs_b[0] = mm(pmt[...], pr_b[0]).astype(BF)
    z_send(zs_b.at[0], zr_b.at[0], 32, 12)
    for j in range(4):
        gate_share(j)
    p_send(ps_g, pr_g, 16, 17)

    owner = lax.div(p, 2) == z
    side = lax.rem(p, 2)
    got(pr_s, prs, 16)
    row = pr_s[...].reshape(32, 8, 128).sum(axis=0)
    row_s[...] = row[4:6]
    row_l[...] = row[0:4]

    def row_copy():
        return pltpu.make_async_remote_copy(
            src_ref=row_l, dst_ref=zr_l.at[z], send_sem=zss.at[18], recv_sem=zrs.at[18],
            device_id=z_id(lax.div(p, 2)), device_id_type=MESH,
        )

    @pl.when(owner)
    def _():
        pltpu.make_async_copy(row_l, zr_l.at[z], zrs.at[18]).start()

    @pl.when(jnp.logical_not(owner))
    def _():
        row_copy().start()

    def cast(d, _):
        pltpu.make_async_remote_copy(
            src_ref=row_s, dst_ref=zr_s.at[z], send_sem=zss.at[16], recv_sem=zrs.at[16],
            device_id=z_id(around(d)), device_id_type=MESH,
        ).start()
        return _

    lax.fori_loop(1, 16, cast, 0)
    pltpu.make_async_copy(row_s, zr_s.at[z], zrs.at[16]).start()
    note(zr_s, zrs, 16)
    note_sent(zr_s, 15, zss.at[16])

    got(pr_b.at[1], prs, 13)
    zs_b[1] = mm(pmt[...], pr_b[1]).astype(BF)
    z_send(zs_b.at[1], zr_b.at[1], 32, 13, 1, SPLIT)
    gterm[...] = nt(nt(bj[...], dpt[...]).astype(BF), w_ref[...])

    got(pr_g, prs, 17)
    tot = pr_g[...].astype(F32).reshape(32, 16, 512).sum(axis=0)
    for t in range(16):
        zs_g[t] = tot[t : t + 1]
    z_send(zs_g, zr_g, 1, 17)
    z_send(zs_b.at[1], zr_b.at[1], 32, 13, SPLIT, 16)

    got(zr_s, zrs, 16)
    for h in range(4):
        few_s[h : h + 1] = zr_s[4 * h : 4 * h + 4, 0:1, :].sum(axis=0) * SCALE
    few_s[4:5] = zr_s[:, 1:2, :].sum(axis=0) * SCALE
    few_s[5:8] = jnp.zeros((3, 128), F32)

    def few(d, _):
        q = lax.rem(p + d * 13, 32)
        pltpu.make_async_remote_copy(
            src_ref=few_s, dst_ref=ar_s.at[p], send_sem=pss.at[18], recv_sem=prs.at[18],
            device_id=p_id(q), device_id_type=MESH,
        ).start()
        return _

    lax.fori_loop(1, 32, few, 0)
    pltpu.make_async_copy(few_s, ar_s.at[p], prs.at[18]).start()
    note_sent(ar_s, 31, pss.at[18])

    def big_copy(t):
        return pltpu.make_async_remote_copy(
            src_ref=big_s, dst_ref=ar_l, send_sem=pss.at[19], recv_sem=prs.at[19],
            device_id={"grp": t, "seq": z * 2 + side}, device_id_type=MESH,
        )

    @pl.when(owner)
    def _():
        got(zr_l, zrs, 18)
        for h in range(4):
            big_s[h * 4 : h * 4 + 4] = zr_l[4 * h : 4 * h + 4].sum(axis=0) * SCALE

        def step(d, _):
            big_copy(lax.rem(g + d, 16)).start()
            return _

        lax.fori_loop(1, 16, step, 0)

    @pl.when(owner & (side == y))
    def _():
        pltpu.make_async_copy(big_s, ar_l, prs.at[19]).start()

    @pl.when(owner & (side != y))
    def _():
        big_copy(g).start()

    got(ar_l, prs, 19)
    sm_ref[0:16] = ar_l[...]
    got(ar_s, prs, 18)
    for a in range(2):
        sm_ref[16 + a * 4 : 20 + a * 4] = ar_s[g * 2 + a, 0:4, :]
    for q in range(32):
        sm_ref[24 + q : 25 + q] = ar_s[q, 4:5, :]

    got(zr_g, zrs, 17)
    row_g[...] = zr_g[...].sum(axis=0) * SCALE

    def rows_out(d, _):
        pltpu.make_async_remote_copy(
            src_ref=row_g, dst_ref=ar_g.at[g], send_sem=pss.at[20], recv_sem=prs.at[20],
            device_id={"grp": lax.rem(g + d, 16)}, device_id_type=MESH,
        ).start()
        return _

    lax.fori_loop(1, 16, rows_out, 0)
    pltpu.make_async_copy(row_g, ar_g.at[g], prs.at[20]).start()
    note_sent(ar_g, 15, pss.at[20])

    got(zr_b.at[0], zrs, 12)
    gterm[...] += nt(bk[:, pair(0)], zr_b[0])
    got(zr_b.at[1], zrs, 13)
    dt_ref[...] = (gterm[...] + nt(bk[:, pair(1)], zr_b[1])).astype(BF)

    got(ar_g, prs, 20)
    for q in range(16):
        gg_ref[q : q + 1] = ar_g[q]

    finish()

    @pl.when(jnp.logical_not(owner))
    def _():
        row_copy().wait_send()

    @pl.when(owner)
    def _():
        for _i in range(15):
            got(big_s, pss, 19)

    @pl.when(owner & (side != y))
    def _():
        got(big_s, pss, 19)


def unpack(dt_ref, gg_ref, sm_ref, d_ref, g_ref, f_ref, m_ref, l_ref):
    d_ref[...] = dt_ref[...].reshape(d_ref.shape)
    g_ref[...] = gg_ref[...]
    for h in range(4):
        l_ref[h] = sm_ref[h * 4 : h * 4 + 4]
        for a in range(2):
            m_ref[h, a * 2 : a * 2 + 1] = sm_ref[16 + a * 4 + h : 17 + a * 4 + h, :64]
            m_ref[h, a * 2 + 1 : a * 2 + 2] = sm_ref[16 + a * 4 + h : 17 + a * 4 + h, 64:]
        f_ref[h] = sm_ref[24:56, h * 32 : h * 32 + 32]


def shards(tokens, cotangent, gate_weight, first_factor, middle_factor, last_factor):
    V = pltpu.VMEM
    big = V((4, 512, 128), BF)
    two = V((2, 512, 256), BF)
    sq = V((512, 512), BF)
    scratch = (
        [V(a.shape, BF) for a in (tokens, cotangent, gate_weight, first_factor, middle_factor, last_factor)]
        + [big, big, two, two] * 2
        + [big] * 4
        + [two] * 4
        + [sq, sq, sq, V((512, 512), F32), sq, sq, sq, sq, sq, sq, sq, sq, V((512, 512), F32)]
        + [V((1024, 1024), BF)] * 2
        + [V((1024, 256), BF)] * 2
        + [V((16, 128, 128), BF)] * 4
        + [V((64, 1024), F32), V((512, 512), F32)]
        + [sq, sq, V((16, 1, 512), F32), V((16, 1, 512), F32), V((1, 512), F32), V((16, 1, 512), F32)]
        + [V((256, 128), F32)] * 2
        + [V((2, 128), F32), V((16, 2, 128), F32), V((4, 128), F32), V((16, 4, 128), F32), V((8, 128), F32), V((32, 8, 128), F32)]
        + [V((16, 128), F32)] * 2
        + [pltpu.SemaphoreType.DMA((n,)) for n in (19, 19, 21, 21, 6)]
        + [pltpu.SemaphoreType.REGULAR((2,))]
    )
    vm = pl.BlockSpec(memory_space=V)
    dt, gg, sm = pl.pallas_call(
        kernel,
        name="mixer",
        out_shape=(
            jax.ShapeDtypeStruct((512, 512), BF),
            jax.ShapeDtypeStruct((16, 512), F32),
            jax.ShapeDtypeStruct((56, 128), F32),
        ),
        in_specs=[pl.BlockSpec(memory_space=pl.ANY)] * 6,
        out_specs=(vm,) * 3,
        scratch_shapes=scratch,
        compiler_params=pltpu.CompilerParams(
            collective_id=0, has_side_effects=True, vmem_limit_bytes=60 * 1024 * 1024
        ),
    )(tokens, cotangent, gate_weight, first_factor, middle_factor, last_factor)
    return pl.pallas_call(
        unpack,
        name="unpack",
        out_shape=(
            jax.ShapeDtypeStruct((32, 4, 4, 512), BF),
            jax.ShapeDtypeStruct((16, 512), F32),
            jax.ShapeDtypeStruct((4, 32, 32), F32),
            jax.ShapeDtypeStruct((4, 4, 64), F32),
            jax.ShapeDtypeStruct((4, 4, 128), F32),
        ),
        in_specs=[vm] * 3,
        out_specs=(vm,) * 5,
    )(dt, gg, sm)


def solution(mesh):
    in_specs = (P(None, "grp", "seq", None), P(None, "grp", "seq", None), P(), P(), P(), P())
    out_specs = (
        P(None, "grp", "seq", None),
        P("seq", None),
        P(),
        P(None, "grp", None),
        P(None, "seq", None),
    )
    return jax.shard_map(shards, mesh=mesh, in_specs=in_specs, out_specs=out_specs, check_vma=False)
```

```python
import jax
import jax.numpy as jnp
from jax import lax
from jax.experimental import pallas as pl
from jax.experimental.pallas import tpu as pltpu
from jax.sharding import PartitionSpec as P

MESH = pl.DeviceIdType.MESH
BF = jnp.bfloat16
F32 = jnp.float32
SCALE = 1.0 / 512.0
HIGH = lax.Precision.HIGHEST
SPLIT = 6


def mm(a, b):
    return jnp.dot(a, b, preferred_element_type=F32)


def tn(a, b):
    return lax.dot_general(a, b, (((0,), (0,)), ((), ())), preferred_element_type=F32)


def nt(a, b):
    return lax.dot_general(a, b, (((1,), (1,)), ((), ())), preferred_element_type=F32)


def exact(a, b):
    return jnp.dot(a, b, preferred_element_type=F32, precision=HIGH)


def grid2(n, m):
    return (
        lax.broadcasted_iota(jnp.int32, (n, m), 0),
        lax.broadcasted_iota(jnp.int32, (n, m), 1),
    )


def onehot(mask, dtype=BF):
    return jnp.where(mask, 1.0, 0.0).astype(dtype)


def swap_lane(m):
    return ((m >> 5) & 3) * 128 + (m >> 7) * 32 + (m & 31)


def kernel(
    x_in, c_in, w_in, ff_in, mf_in, lf_in,
    dt_ref, gg_ref, sm_ref,
    x_ref, c_ref, w_ref, ff_ref, mf_ref, lf_ref,
    zs_f, zr_f, zs_d, zr_d, ps_f, pr_f, ps_d, pr_d,
    ps_m, pr_m, zs_m, zr_m, ps_b, pr_b, zs_b, zr_b,
    xn, xtj, ctj, gate, bk, bj, pm, pmt, pkj, mid, dpt, xtp, gterm,
    aj, ajt, loj, dj, xg, fog, mbg, lbg, gfold, gacc,
    ps_g, pr_g, zs_g, zr_g, row_g, ar_g,
    ps_s, pr_s, row_s, zr_s, row_l, zr_l, few_s, ar_s, big_s, ar_l,
    zss, zrs, pss, prs, ins, far,
):
    g = lax.axis_index("grp")
    s = lax.axis_index("seq")
    z = lax.div(s, 2)
    y = lax.rem(s, 2)
    p = y * 16 + g
    head = lax.div(z, 4)

    def z_id(t):
        return {"seq": t * 2 + y}

    def p_id(q):
        return {"grp": lax.rem(q, 16), "seq": z * 2 + lax.div(q, 16)}

    def around(d):
        return lax.rem(z + d, 16)

    loads = [
        pltpu.make_async_copy(src, dst, ins.at[n])
        for n, (src, dst) in enumerate(
            ((x_in, x_ref), (c_in, c_ref), (w_in, w_ref), (ff_in, ff_ref), (mf_in, mf_ref), (lf_in, lf_ref))
        )
    ]
    loads[0].start()
    bar = pltpu.get_barrier_semaphore()
    waiting, leaving = {}, []

    def greet_z(d, _):
        pl.semaphore_signal(bar, inc=1, device_id=z_id(around(d)), device_id_type=MESH)
        return _

    def greet_p(d, _):
        pl.semaphore_signal(bar, inc=1, device_id=p_id(lax.rem(p + d, 32)), device_id_type=MESH)
        return _

    lax.fori_loop(1, 5, greet_z, 0)
    lax.fori_loop(12, 16, greet_z, 0)
    lax.fori_loop(1, 32, greet_p, 0)

    def block(t, rows):
        return pl.ds(pl.multiple_of(t * rows, rows), rows)

    def z_send(src, dst, rows, k, first=1, last=16, stop=None):
        def step(d, _):
            t = around(d * 7)
            pltpu.make_async_remote_copy(
                src_ref=src.at[block(t, rows)], dst_ref=dst.at[block(z, rows)],
                send_sem=zss.at[k], recv_sem=zrs.at[k],
                device_id=z_id(t), device_id_type=MESH,
            ).start()
            return _

        lax.fori_loop(first, last if stop is None else stop, step, 0)
        if last < 16:
            return
        pltpu.make_async_copy(src.at[block(z, rows)], dst.at[block(z, rows)], zrs.at[k]).start()
        note(dst, zrs, k)
        note_sent(src, 15 * rows, zss.at[k])

    def p_send(src, dst, rows, k):
        def step(d, _):
            q = lax.rem(p + d * 13, 32)
            pltpu.make_async_remote_copy(
                src_ref=src.at[block(q, rows)], dst_ref=dst.at[block(p, rows)],
                send_sem=pss.at[k], recv_sem=prs.at[k],
                device_id=p_id(q), device_id_type=MESH,
            ).start()
            return _

        lax.fori_loop(1, 32, step, 0)
        pltpu.make_async_copy(src.at[block(p, rows)], dst.at[block(p, rows)], prs.at[k]).start()
        note(dst, prs, k)
        note_sent(src, 31 * rows, pss.at[k])

    def got(dst, sem, n):
        pltpu.make_async_copy(dst, dst, sem.at[n]).wait()
        waiting.pop((id(sem), n), None)

    def note(dst, sem, n):
        waiting[(id(sem), n)] = lambda: got(dst, sem, n)

    def note_sent(src, n, sem):
        part = src.at[pl.ds(0, n)]
        leaving.append(pltpu.make_async_copy(part, part, sem))

    def finish():
        for step in list(waiting.values()):
            step()
        for copy in leaving:
            copy.wait()

    def z_pair(src, dst, k):
        def step(d, _):
            for t in (around(d), around(16 - d)):
                pltpu.make_async_remote_copy(
                    src_ref=src.at[block(t, 32)], dst_ref=dst.at[block(z, 32)],
                    send_sem=zss.at[k], recv_sem=zrs.at[k],
                    device_id=z_id(t), device_id_type=MESH,
                ).start()
            return _

        return step

    def pair(k):
        return slice(k * 256, k * 256 + 256)

    def lanes(j):
        return slice(j * 128, j * 128 + 128)

    def half(yy):
        return slice(yy * 256, yy * 256 + 256)

    r, c = grid2(512, 512)
    bk[...] = onehot(r == (c & 31) * 16 + ((c >> 5) & 3) * 4 + (c >> 7))
    loads[0].wait()
    for load in loads[1:]:
        load.start()
    xn[...] = x_ref[...].reshape(512, 512)
    def turn(h):
        part = tn(xn[...], bk[:, pair(h)]).astype(BF)
        for k in range(2):
            zs_f[2 * h + k] = part[:, lanes(k)]

    turn(0)
    pl.semaphore_wait(bar, 39)
    pl.semaphore_signal(far.at[0], inc=1, device_id=z_id(around(4)), device_id_type=MESH)
    pl.semaphore_signal(far.at[1], inc=1, device_id=z_id(around(12)), device_id_type=MESH)
    for k in range(2):
        lax.fori_loop(1, 5, z_pair(zs_f.at[k], zr_f.at[k], k), 0)
    turn(1)
    pl.semaphore_wait(far.at[0], 1)
    pl.semaphore_wait(far.at[1], 1)
    for k in range(2):
        lax.fori_loop(5, 8, z_pair(zs_f.at[k], zr_f.at[k], k), 0)
        z_send(zs_f.at[k], zr_f.at[k], 32, k, 8, 16, 9)
    for k in range(2, 4):
        z_send(zs_f.at[k], zr_f.at[k], 32, k)

    bj[...] = onehot(r == (c & 31) * 16 + (c >> 7) * 4 + ((c >> 5) & 3))
    xtj[...] = tn(xn[...], bj[...]).astype(BF)
    loads[1].wait()
    ctj[...] = tn(c_ref[...].reshape(512, 512), bj[...]).astype(BF)
    loads[2].wait()
    gt = jax.nn.sigmoid(tn(w_ref[...], xtj[...]))
    gate[...] = gt
    dmix = (ctj[...].astype(F32) * gt).astype(BF)
    for k in range(2):
        zs_d[k] = dmix[:, pair(k)]
    for k in range(2):
        z_send(zs_d.at[k], zr_d.at[k], 32, 4 + k)

    pm[...] = onehot(c == (r & 15) * 32 + (r >> 4))
    pmt[...] = onehot(r == (c & 15) * 32 + (c >> 4))
    pkj[...] = onehot(r == swap_lane(c))
    r4, c4 = grid2(128, 32)
    spread4 = onehot((r4 & 31) == c4)
    r1, c1 = grid2(128, 128)
    same4 = (r1 >> 5) == (c1 >> 5)
    for load in loads[3:]:
        load.wait()
    ff = ff_ref[head]
    fk = jnp.where(same4, nt(mm(spread4, ff).astype(BF), spread4), 0.0).astype(BF)
    fkt = jnp.where(same4, nt(nt(spread4, ff).astype(BF), spread4), 0.0).astype(BF)
    qk = onehot(c1 == (r1 & 15) * 8 + ((r1 >> 4) & 1) * 4 + (r1 >> 5))
    lf = lf_ref[head]
    lp = nt(mm(qk, lf).astype(BF), qk).astype(BF)
    lpt = nt(nt(qk, lf).astype(BF), qk).astype(BF)
    rj, cj = grid2(1024, 64)
    spread_j = onehot(cj == ((rj >> 4) & 15) * 4 + (rj >> 8))
    mf = mf_ref[head]
    wide = mm(spread_j, mf).astype(BF)
    wide_t = nt(spread_j, mf).astype(BF)
    for b in range(4):
        rb, cb = grid2(256, 1024)
        same16 = (rb & 15) == (cb & 15)
        aj[half(b)] = jnp.where(same16, nt(wide[half(b)], spread_j), 0.0).astype(BF)
        ajt[half(b)] = jnp.where(same16, nt(wide_t[half(b)], spread_j), 0.0).astype(BF)
    xtp[...] = mm(pm[...], xtj[...]).astype(BF)

    for k in range(4):
        got(zr_f.at[k], zrs, k)
        ps_f[k] = mm(pm[...], zr_f[k]).astype(BF)
        p_send(ps_f.at[k], pr_f.at[k], 16, k)

    for k in range(4):
        got(pr_f.at[k], prs, k)
        fo = mm(pr_f[k], fkt).astype(BF)
        for yy in range(2):
            at = (k * 2 + yy) * 16
            fog[:, at : at + 16, :] = fo[half(yy)].reshape(16, 16, 128)
    for gi in range(16):
        lbg[gi] = mm(lp, fog[gi]).astype(BF)
    for k in range(4):
        for yy in range(2):
            at = (k * 2 + yy) * 16
            mid[half(yy), lanes(k)] = lbg[:, at : at + 16, :].reshape(256, 128)
    lo = mm(mid[...], pkj[...]).astype(BF)
    for j in range(4):
        for yy in range(2):
            loj[half(j), lanes(yy)] = lo[half(yy), lanes(j)]
    for j in range(4):
        mx = mm(aj[half(j)], loj[...]).astype(BF)
        for yy in range(2):
            ps_m[j, half(yy)] = mx[:, lanes(yy)]
        p_send(ps_m.at[j], pr_m.at[j], 16, 4 + j)

    def d_relay(j):
        got(zr_d.at[j], zrs, 4 + j)
        ps_d[j] = mm(pm[...], zr_d[j]).astype(BF)
        p_send(ps_d.at[j], pr_d.at[j], 16, 8 + j)

    def m_relay(j):
        got(pr_m.at[j], prs, 4 + j)
        zs_m[j] = mm(pmt[...], pr_m[j]).astype(BF)
        z_send(zs_m.at[j], zr_m.at[j], 32, 8 + j)

    d_relay(0)
    m_relay(0)
    m_relay(1)
    m_relay(2)
    d_relay(1)
    m_relay(3)

    for k in range(2):
        got(pr_d.at[k], prs, 8 + k)
        for j in range(2):
            for yy in range(2):
                dj[half(2 * k + j), lanes(yy)] = pr_d[k, half(yy), lanes(j)]
    mb = mm(ajt[...], dj[...]).astype(BF)
    for j in range(4):
        for yy in range(2):
            mid[half(yy), lanes(j)] = mb[half(j), lanes(yy)]
    mbk = mm(mid[...], pkj[...]).astype(BF)
    for k in range(4):
        for yy in range(2):
            at = (k * 2 + yy) * 16
            mbg[:, at : at + 16, :] = mbk[half(yy), lanes(k)].reshape(16, 16, 128)
    for gi in range(16):
        lbg[gi] = mm(lpt, mbg[gi]).astype(BF)
    fb = mm(lbg[...].reshape(2048, 128), fk).astype(BF).reshape(16, 128, 128)
    for k in range(4):
        for yy in range(2):
            at = (k * 2 + yy) * 16
            ps_b[k // 2, half(yy), lanes(k % 2)] = fb[:, at : at + 16, :].reshape(256, 128)
    p_send(ps_b.at[0], pr_b.at[0], 16, 12)

    for k in range(4):
        for yy in range(2):
            at = (k * 2 + yy) * 16
            xg[:, at : at + 16, :] = pr_f[k, half(yy)].reshape(16, 16, 128)
    for b in range(4):
        rb, cb = grid2(256, 1024)
        gram = nt(dj[half(b)], loj[...])
        gram = jnp.where((rb & 15) == (cb & 15), gram, 0.0)
        gfold[b * 16 : b * 16 + 16] = gram.reshape(16, 16, 1024).sum(axis=1)
    gm = exact(gfold[...], onehot(cj == ((rj >> 4) & 15) * 4 + (rj >> 8), F32))
    gl = jnp.zeros((128, 128), F32)
    gf = jnp.zeros((128, 128), F32)
    for gi in range(16):
        gl = gl + nt(mbg[gi], fog[gi])
        gf = gf + tn(lbg[gi], xg[gi])
    ra, ca = grid2(256, 128)
    pa, aa = ra >> 3, ra & 7
    kc = (ca & 15) * 8 + ((ca >> 4) & 1) * 4 + (ca >> 5)
    sel_l = onehot((aa < 4) & (kc == pa * 4 + aa), F32)
    pack = exact(sel_l, exact(gl, qk.astype(F32)))
    rm, cm = grid2(256, 64)
    jm = (cm & 15) * 4 + (cm >> 4)
    i64r, i64c = grid2(64, 128)
    for odd in range(2):
        sel_m = onehot(((rm & 7) == 4) & (jm == (rm >> 3) * 2 + odd), F32)
        pack = pack + exact(exact(sel_m, gm), onehot(i64c == i64r + 64 * odd, F32))
    sel_f = onehot((aa == 5) & ((ca & 31) == pa), F32)
    fold_c = onehot(c1 == (r1 & 31) + head * 32, F32)
    pack = pack + exact(exact(sel_f, jnp.where(same4, gf, 0.0)), fold_c)
    ps_s[...] = pack
    p_send(ps_s, pr_s, 8, 16)
    p_send(ps_b.at[1], pr_b.at[1], 16, 13)

    def gate_share(j):
        got(zr_m.at[j], zrs, 8 + j)
        gt = gate[:, lanes(j)]
        dpre = (ctj[:, lanes(j)].astype(F32) * zr_m[j].astype(F32) * gt * (1.0 - gt)).astype(BF)
        dpt[:, lanes(j)] = dpre
        share = nt(xtp[:, lanes(j)], dpre)
        if j == 0:
            gacc[...] = share
        elif j < 3:
            gacc[...] += share
        else:
            ps_g[...] = (gacc[...] + share).astype(BF)

    got(pr_b.at[0], prs, 12)
    zs_b[0] = mm(pmt[...], pr_b[0]).astype(BF)
    z_send(zs_b.at[0], zr_b.at[0], 32, 12)
    for j in range(4):
        gate_share(j)
    p_send(ps_g, pr_g, 16, 17)

    owner = lax.div(p, 2) == z
    side = lax.rem(p, 2)
    got(pr_s, prs, 16)
    row = pr_s[...].reshape(32, 8, 128).sum(axis=0)
    row_s[...] = row[4:6]
    row_l[...] = row[0:4]

    def row_copy():
        return pltpu.make_async_remote_copy(
            src_ref=row_l, dst_ref=zr_l.at[z], send_sem=zss.at[18], recv_sem=zrs.at[18],
            device_id=z_id(lax.div(p, 2)), device_id_type=MESH,
        )

    @pl.when(owner)
    def _():
        pltpu.make_async_copy(row_l, zr_l.at[z], zrs.at[18]).start()

    @pl.when(jnp.logical_not(owner))
    def _():
        row_copy().start()

    def cast(d, _):
        pltpu.make_async_remote_copy(
            src_ref=row_s, dst_ref=zr_s.at[z], send_sem=zss.at[16], recv_sem=zrs.at[16],
            device_id=z_id(around(d)), device_id_type=MESH,
        ).start()
        return _

    lax.fori_loop(1, 16, cast, 0)
    pltpu.make_async_copy(row_s, zr_s.at[z], zrs.at[16]).start()
    note(zr_s, zrs, 16)
    note_sent(zr_s, 15, zss.at[16])

    got(pr_b.at[1], prs, 13)
    zs_b[1] = mm(pmt[...], pr_b[1]).astype(BF)
    z_send(zs_b.at[1], zr_b.at[1], 32, 13, 1, SPLIT)
    gterm[...] = nt(nt(bj[...], dpt[...]).astype(BF), w_ref[...])

    got(pr_g, prs, 17)
    tot = pr_g[...].astype(F32).reshape(32, 16, 512).sum(axis=0)
    for t in range(16):
        zs_g[t] = tot[t : t + 1]
    z_send(zs_g, zr_g, 1, 17)
    z_send(zs_b.at[1], zr_b.at[1], 32, 13, SPLIT, 16)

    got(zr_s, zrs, 16)
    for h in range(4):
        few_s[h : h + 1] = zr_s[4 * h : 4 * h + 4, 0:1, :].sum(axis=0) * SCALE
    few_s[4:5] = zr_s[:, 1:2, :].sum(axis=0) * SCALE
    few_s[5:8] = jnp.zeros((3, 128), F32)

    def few(d, _):
        q = lax.rem(p + d * 13, 32)
        pltpu.make_async_remote_copy(
            src_ref=few_s, dst_ref=ar_s.at[p], send_sem=pss.at[18], recv_sem=prs.at[18],
            device_id=p_id(q), device_id_type=MESH,
        ).start()
        return _

    lax.fori_loop(1, 32, few, 0)
    pltpu.make_async_copy(few_s, ar_s.at[p], prs.at[18]).start()
    note_sent(ar_s, 31, pss.at[18])

    def big_copy(t):
        return pltpu.make_async_remote_copy(
            src_ref=big_s, dst_ref=ar_l, send_sem=pss.at[19], recv_sem=prs.at[19],
            device_id={"grp": t, "seq": z * 2 + side}, device_id_type=MESH,
        )

    @pl.when(owner)
    def _():
        got(zr_l, zrs, 18)
        for h in range(4):
            big_s[h * 4 : h * 4 + 4] = zr_l[4 * h : 4 * h + 4].sum(axis=0) * SCALE

        def step(d, _):
            big_copy(lax.rem(g + d, 16)).start()
            return _

        lax.fori_loop(1, 16, step, 0)

    @pl.when(owner & (side == y))
    def _():
        pltpu.make_async_copy(big_s, ar_l, prs.at[19]).start()

    @pl.when(owner & (side != y))
    def _():
        big_copy(g).start()

    got(ar_l, prs, 19)
    sm_ref[0:16] = ar_l[...]
    got(ar_s, prs, 18)
    for a in range(2):
        sm_ref[16 + a * 4 : 20 + a * 4] = ar_s[g * 2 + a, 0:4, :]
    for q in range(32):
        sm_ref[24 + q : 25 + q] = ar_s[q, 4:5, :]

    got(zr_g, zrs, 17)
    row_g[...] = zr_g[...].sum(axis=0) * SCALE

    def rows_out(d, _):
        pltpu.make_async_remote_copy(
            src_ref=row_g, dst_ref=ar_g.at[g], send_sem=pss.at[20], recv_sem=prs.at[20],
            device_id={"grp": lax.rem(g + d, 16)}, device_id_type=MESH,
        ).start()
        return _

    lax.fori_loop(1, 16, rows_out, 0)
    pltpu.make_async_copy(row_g, ar_g.at[g], prs.at[20]).start()
    note_sent(ar_g, 15, pss.at[20])

    got(zr_b.at[0], zrs, 12)
    gterm[...] += nt(bk[:, pair(0)], zr_b[0])
    got(zr_b.at[1], zrs, 13)
    dt_ref[...] = (gterm[...] + nt(bk[:, pair(1)], zr_b[1])).astype(BF)

    got(ar_g, prs, 20)
    for q in range(16):
        gg_ref[q : q + 1] = ar_g[q]

    finish()

    @pl.when(jnp.logical_not(owner))
    def _():
        row_copy().wait_send()

    @pl.when(owner)
    def _():
        for _i in range(15):
            got(big_s, pss, 19)

    @pl.when(owner & (side != y))
    def _():
        got(big_s, pss, 19)


def unpack(dt_ref, gg_ref, sm_ref, d_ref, g_ref, f_ref, m_ref, l_ref):
    d_ref[...] = dt_ref[...].reshape(d_ref.shape)
    g_ref[...] = gg_ref[...]
    for h in range(4):
        l_ref[h] = sm_ref[h * 4 : h * 4 + 4]
        for a in range(2):
            m_ref[h, a * 2 : a * 2 + 1] = sm_ref[16 + a * 4 + h : 17 + a * 4 + h, :64]
            m_ref[h, a * 2 + 1 : a * 2 + 2] = sm_ref[16 + a * 4 + h : 17 + a * 4 + h, 64:]
        f_ref[h] = sm_ref[24:56, h * 32 : h * 32 + 32]


def shards(tokens, cotangent, gate_weight, first_factor, middle_factor, last_factor):
    V = pltpu.VMEM
    big = V((4, 512, 128), BF)
    two = V((2, 512, 256), BF)
    sq = V((512, 512), BF)
    scratch = (
        [V(a.shape, BF) for a in (tokens, cotangent, gate_weight, first_factor, middle_factor, last_factor)]
        + [big, big, two, two] * 2
        + [big] * 4
        + [two] * 4
        + [sq, sq, sq, V((512, 512), F32), sq, sq, sq, sq, sq, sq, sq, sq, V((512, 512), F32)]
        + [V((1024, 1024), BF)] * 2
        + [V((1024, 256), BF)] * 2
        + [V((16, 128, 128), BF)] * 4
        + [V((64, 1024), F32), V((512, 512), F32)]
        + [sq, sq, V((16, 1, 512), F32), V((16, 1, 512), F32), V((1, 512), F32), V((16, 1, 512), F32)]
        + [V((256, 128), F32)] * 2
        + [V((2, 128), F32), V((16, 2, 128), F32), V((4, 128), F32), V((16, 4, 128), F32), V((8, 128), F32), V((32, 8, 128), F32)]
        + [V((16, 128), F32)] * 2
        + [pltpu.SemaphoreType.DMA((n,)) for n in (19, 19, 21, 21, 6)]
        + [pltpu.SemaphoreType.REGULAR((2,))]
    )
    vm = pl.BlockSpec(memory_space=V)
    dt, gg, sm = pl.pallas_call(
        kernel,
        name="mixer",
        out_shape=(
            jax.ShapeDtypeStruct((512, 512), BF),
            jax.ShapeDtypeStruct((16, 512), F32),
            jax.ShapeDtypeStruct((56, 128), F32),
        ),
        in_specs=[pl.BlockSpec(memory_space=pl.ANY)] * 6,
        out_specs=(vm,) * 3,
        scratch_shapes=scratch,
        compiler_params=pltpu.CompilerParams(
            collective_id=0, has_side_effects=True, vmem_limit_bytes=60 * 1024 * 1024
        ),
    )(tokens, cotangent, gate_weight, first_factor, middle_factor, last_factor)
    return pl.pallas_call(
        unpack,
        name="unpack",
        out_shape=(
            jax.ShapeDtypeStruct((32, 4, 4, 512), BF),
            jax.ShapeDtypeStruct((16, 512), F32),
            jax.ShapeDtypeStruct((4, 32, 32), F32),
            jax.ShapeDtypeStruct((4, 4, 64), F32),
            jax.ShapeDtypeStruct((4, 4, 128), F32),
        ),
        in_specs=[vm] * 3,
        out_specs=(vm,) * 5,
    )(dt, gg, sm)


def solution(mesh):
    in_specs = (P(None, "grp", "seq", None), P(None, "grp", "seq", None), P(), P(), P(), P())
    out_specs = (
        P(None, "grp", "seq", None),
        P("seq", None),
        P(),
        P(None, "grp", None),
        P(None, "seq", None),
    )
    return jax.shard_map(shards, mesh=mesh, in_specs=in_specs, out_specs=out_specs, check_vma=False)
```
